256 devices in a mesh: alpha: 128 (over y, z, x), beta: 2 (over core).
Axes of the slice: x: 4, y: 4, z: 8, core: 2. Of those that a mesh axis runs over, the one named last changes fastest.
Arguments:
- coeffs: bfloat16 [1, 16384, 4096], P(None, 'alpha', 'beta'), may hold values from -6 to 6
- beta_list: int32 [32, 8], P('beta'), may hold values from 0 to 31
- beta_kind: int32 [32, 8], P('beta'), may hold values from 0 to 7
- opp_beta_kind: int32 [32, 8], P('beta'), may hold values from 0 to 7
- alpha_list: int32 [128, 4], replicated, may hold values from 0 to 127, as said below
- alpha_kind: int32 [128, 4], replicated, may hold values from 0 to 7
- opp_list: int32 [128, 3], replicated, may hold values from 0 to 127, as said below
- opp_kind: int32 [128, 3], replicated, may hold values from 0 to 7
- beta_table: bfloat16 [8, 128, 128], replicated, may hold values from -0.1875 to 0.1875
- alpha_table: bfloat16 [8, 128, 128], replicated, may hold values from -0.25 to 0.25
- opp_alpha_table: bfloat16 [8, 128, 128], replicated, may hold values from -0.3125 to 0.3125
- opp_beta_table: bfloat16 [8, 128, 128], replicated, may hold values from -0.1875 to 0.1875
Outputs:
- sigma_out: bfloat16 [1, 16384, 4096], P(None, 'alpha', 'beta')
The draws below stay inside these ranges and needn't reach their ends.
Inputs may be any that keep to these rules, and one draw needn't show every extreme that they name: `alpha_list`: each entry of row i lies within 3 of i; the entries of a row are distinct. `opp_list`: each entry of row i lies within 3 of i; the entries of a row are distinct.
All inputs are finite; a program needn't handle non-finite values.
Results may differ from the reference program's by a relative error of at most 0.0034.
Values may be sent and summed in bfloat16 or wider, within the bound.
No kernel may reach another device: no remote copies, remote signals or barrier semaphores. Data moves between devices by JAX's collectives and lax.ppermute only.
A program may use at most 128 MiB of HBM per device.

```python
import jax
import jax.numpy as jnp
from jax import lax

TILE = 128
NB = 4096
ROOTS = 1
BETA_LINKS = 8
ALPHA_LINKS = 4
OPP_LINKS = 3
KINDS = 8
REACH = 3
NA = 16384


def pick_nearby(key, count):
    block_count = NA // TILE
    span_count = 2 * REACH + 1
    offsets = jnp.arange(span_count, dtype=jnp.int32) - REACH
    row_ids = jnp.arange(block_count, dtype=jnp.int32)[:, None]
    target = row_ids + offsets[None, :]
    inside = (target >= 0) & (target < block_count)
    scores = jax.random.randint(key, (block_count, span_count), 0, 1 << 20, dtype=jnp.int32) * span_count + jnp.arange(span_count, dtype=jnp.int32)[None, :]
    scores = jnp.where(inside, scores + 1, 0)
    unused, chosen = lax.top_k(scores, count)
    return jnp.take_along_axis(target, chosen, axis=1).astype(jnp.int32)


def draw_alpha_list(key, part):
    return pick_nearby(jax.random.fold_in(key, 11), ALPHA_LINKS)


def draw_opp_list(key, part):
    return pick_nearby(jax.random.fold_in(key, 23), OPP_LINKS)


def set_ends(array, own_key, smallest, high):
    longest = array.shape.index(max(array.shape))
    spots = []
    for shift in (0, 1):
        where = [jax.random.randint(jax.random.fold_in(own_key, axis), (), 0, length) for axis, length in enumerate(array.shape)]
        where[longest] = (where[longest] + shift) % array.shape[longest]
        spots.append(tuple(where))
    return array.at[spots[0]].set(smallest).at[spots[1]].set(high)


def block_scale(own_key, shape, pieces, least, top_value):
    def one(dim, parts):
        heights = jax.random.uniform(jax.random.fold_in(jax.random.fold_in(own_key, 6), dim), (parts,), jnp.float32, least / len(pieces), top_value / len(pieces))
        return jnp.repeat(jnp.exp(heights), shape[dim] // parts).reshape((-1,) + (1,) * (len(shape) - dim - 1))

    level = one(*pieces[0])
    for cut in pieces[1:]:
        level = level * one(*cut)
    return level


def normal_values(own_key, extent, spread, limit, split=(), kind=jnp.bfloat16):
    drawn = jax.random.normal(own_key, extent, jnp.float32) * spread
    if len(split) > 0:
        drawn = block_scale(own_key, extent, split, -0.22, 0.18) * drawn
    return jnp.clip(drawn, min=-limit, max=limit).astype(kind)


def setup_inputs(seed: int = 0) -> dict:
    keys = jax.random.split(jax.random.key(seed), 13)
    return {
        "coeffs": normal_values(keys[0], (ROOTS, NA, NB), 1.0, 6.0, ((1, 128), (2, 2))),
        "beta_list": set_ends(jax.random.randint(keys[1], (NB // TILE, BETA_LINKS), 0, NB // TILE), jax.random.fold_in(keys[1], 1), 0, (NB // TILE) - 1).astype(jnp.int32),
        "beta_kind": set_ends(jax.random.randint(keys[2], (NB // TILE, BETA_LINKS), 0, KINDS), jax.random.fold_in(keys[2], 1), 0, KINDS - 1).astype(jnp.int32),
        "opp_beta_kind": set_ends(jax.random.randint(keys[3], (NB // TILE, BETA_LINKS), 0, KINDS), jax.random.fold_in(keys[3], 1), 0, KINDS - 1).astype(jnp.int32),
        "alpha_list": draw_alpha_list(jax.random.fold_in(keys[12], 71), 0),
        "alpha_kind": set_ends(jax.random.randint(keys[5], (NA // TILE, ALPHA_LINKS), 0, KINDS), jax.random.fold_in(keys[5], 1), 0, KINDS - 1).astype(jnp.int32),
        "opp_list": draw_opp_list(jax.random.fold_in(keys[12], 71), 0),
        "opp_kind": set_ends(jax.random.randint(keys[7], (NA // TILE, OPP_LINKS), 0, KINDS), jax.random.fold_in(keys[7], 1), 0, KINDS - 1).astype(jnp.int32),
        "beta_table": normal_values(keys[8], (KINDS, TILE, TILE), (TILE * BETA_LINKS) ** -0.5, 0.1875),
        "alpha_table": normal_values(keys[9], (KINDS, TILE, TILE), (TILE * ALPHA_LINKS) ** -0.5, 0.25),
        "opp_alpha_table": normal_values(keys[10], (KINDS, TILE, TILE), (TILE * OPP_LINKS) ** -0.5, 0.3125),
        "opp_beta_table": normal_values(keys[11], (KINDS, TILE, TILE), (TILE * BETA_LINKS) ** -0.5, 0.1875),
    }


def beta_apply(row_data, sources, kind_ids, tile_table):
    root_count, row_count, col_count = row_data.shape
    tile_size = tile_table.shape[1]
    tiled = row_data.reshape(root_count, row_count, col_count // tile_size, tile_size)
    summed = jnp.zeros((root_count, row_count, sources.shape[0], tile_size), jnp.float32)
    for link in range(sources.shape[1]):
        picked = jnp.take(tiled, sources[:, link], axis=2).astype(jnp.float32)
        tile_sets = jnp.take(tile_table, kind_ids[:, link], axis=0).astype(jnp.float32)
        summed = summed + jnp.einsum("rajt,jst->rajs", picked, tile_sets, precision=lax.Precision.HIGHEST)
    return summed.reshape(root_count, row_count, -1)


def alpha_sum(blocks, sources, kind_ids, tile_table):
    summed = jnp.zeros((blocks.shape[0], blocks.shape[2], blocks.shape[3]), jnp.float32)
    for link in range(sources.shape[0]):
        picked = lax.dynamic_index_in_dim(blocks, sources[link], 1, keepdims=False).astype(jnp.float32)
        tile_one = lax.dynamic_index_in_dim(tile_table, kind_ids[link], 0, keepdims=False).astype(jnp.float32)
        summed = summed + jnp.einsum("st,rtc->rsc", tile_one, picked, precision=lax.Precision.HIGHEST)
    return summed


def reference(coeffs, beta_list, beta_kind, opp_beta_kind, alpha_list, alpha_kind, opp_list, opp_kind, beta_table, alpha_table, opp_alpha_table, opp_beta_table):
    root_count, alpha_count, beta_count = coeffs.shape
    tile_size = alpha_table.shape[1]
    block_count = alpha_count // tile_size
    blocks = coeffs.reshape(root_count, block_count, tile_size, beta_count)

    def one_block(block):
        own_rows = lax.dynamic_index_in_dim(blocks, block, 1, keepdims=False)
        beta_part = beta_apply(own_rows, beta_list, beta_kind, beta_table)
        alpha_part = alpha_sum(blocks, alpha_list[block], alpha_kind[block], alpha_table)
        half_sum = alpha_sum(blocks, opp_list[block], opp_kind[block], opp_alpha_table).astype(jnp.bfloat16)
        mixed_part = beta_apply(half_sum, beta_list, opp_beta_kind, opp_beta_table)
        return (beta_part + alpha_part + mixed_part).astype(jnp.bfloat16)

    result = lax.map(one_block, jnp.arange(block_count, dtype=jnp.int32))
    return jnp.transpose(result, (1, 0, 2, 3)).reshape(root_count, alpha_count, beta_count)
```

```python
import functools

import jax
import jax.numpy as jnp
from jax import lax
from jax.experimental import pallas as pl
from jax.experimental.pallas import tpu as pltpu
from jax.sharding import Mesh, PartitionSpec as P

REACH = 3
RING = 4
TILE = 128
ANY = pl.BlockSpec(memory_space=pl.ANY)
SMEM = pl.BlockSpec(memory_space=pltpu.SMEM)
VMEM = pl.BlockSpec(memory_space=pltpu.VMEM)
LIMIT = 48 << 20


def cost(flops, moved):
    return pl.CostEstimate(flops=flops, bytes_accessed=moved, transcendentals=0)


def run_all(copies):
    for copy in copies:
        copy.start()
    for copy in copies:
        copy.wait()


def cut_kernel(place, whole, *rest):
    pieces, sems = rest[:RING], rest[RING]
    width = whole.shape[1] // RING
    copies = []
    for d in range(RING):
        quarter = lax.rem(place[0] + d, RING)
        cols = pl.ds(pl.multiple_of(quarter * width, width), width)
        copies.append(pltpu.make_async_copy(whole.at[:, cols], pieces[d], sems.at[d]))
    run_all(copies)


def cut(place, whole):
    rows, cols = whole.shape
    piece = jax.ShapeDtypeStruct((rows, cols // RING), whole.dtype)
    return pl.pallas_call(
        cut_kernel,
        out_shape=[piece] * RING,
        in_specs=[SMEM, ANY],
        out_specs=[ANY] * RING,
        scratch_shapes=[pltpu.SemaphoreType.DMA((RING,))],
        cost_estimate=cost(0, 4 * rows * cols),
        name="cut",
    )(place, whole)


def edge_kernel(place, p0, p1, p2, p3, up, down, sems):
    pieces = (p0, p1, p2, p3)
    for d in range(RING):
        block = lax.rem(place[0] - d + RING, RING)

        @pl.when(block > 0)
        def _():
            pltpu.make_async_copy(pieces[d], up.at[block - 1], sems.at[0, d]).start()

        @pl.when(block < RING - 1)
        def _():
            pltpu.make_async_copy(pieces[d], down.at[block], sems.at[1, d]).start()

    for d in range(RING):
        block = lax.rem(place[0] - d + RING, RING)

        @pl.when(block > 0)
        def _():
            pltpu.make_async_copy(pieces[d], up.at[block - 1], sems.at[0, d]).wait()

        @pl.when(block < RING - 1)
        def _():
            pltpu.make_async_copy(pieces[d], down.at[block], sems.at[1, d]).wait()


def edges(place, pieces):
    rows, cols = pieces[0].shape
    part = jax.ShapeDtypeStruct((REACH, rows, cols), pieces[0].dtype)
    return pl.pallas_call(
        edge_kernel,
        out_shape=[part] * 2,
        in_specs=[SMEM] + [ANY] * RING,
        out_specs=[ANY] * 2,
        scratch_shapes=[pltpu.SemaphoreType.DMA((2, RING))],
        cost_estimate=cost(0, 4 * REACH * rows * cols * 2),
        name="edges",
    )(place, *pieces)


def near_kernel(links, place, sources, kinds, p0, p1, p2, p3, above, below, table, *rest):
    outs, (held, sems) = rest[:RING], rest[RING:]
    copies = [
        pltpu.make_async_copy(above, held.at[pl.ds(0, REACH)], sems.at[4]),
        pltpu.make_async_copy(below, held.at[pl.ds(REACH + RING, REACH)], sems.at[5]),
    ]
    for d, piece in enumerate((p0, p1, p2, p3)):
        block = lax.rem(place[0] - d + RING, RING)
        copies.append(pltpu.make_async_copy(piece, held.at[REACH + block], sems.at[d]))
    run_all(copies)
    for d in range(RING):
        block = place[1] * RING + lax.rem(place[0] + d, RING)
        total = None
        for m in range(links):
            at = sources[block, m] - place[1] * RING + REACH
            term = jnp.dot(
                table[kinds[block, m]], held[at], preferred_element_type=jnp.float32
            )
            total = term if total is None else total + term
        outs[d][...] = total.astype(outs[d].dtype)


def near(place, sources, kinds, pieces, above, below, table, name):
    rows, cols = pieces[0].shape
    links = sources.shape[1]
    piece = jax.ShapeDtypeStruct((rows, cols), pieces[0].dtype)
    return pl.pallas_call(
        functools.partial(near_kernel, links),
        out_shape=[piece] * RING,
        in_specs=[SMEM] * 3 + [ANY] * (RING + 2) + [VMEM],
        out_specs=[VMEM] * RING,
        scratch_shapes=[
            pltpu.VMEM((RING + 2 * REACH, rows, cols), pieces[0].dtype),
            pltpu.SemaphoreType.DMA((RING + 2,)),
        ],
        cost_estimate=cost(2 * RING * links * rows * rows * cols, 14 * 2 * rows * cols),
        compiler_params=pltpu.CompilerParams(vmem_limit_bytes=LIMIT),
        name=name,
    )(place, sources, kinds, *pieces, above, below, table)


def far_kernel(count, links, slots, sources, kinds, *rest):
    pieces, table = rest[:count], rest[count]
    if len(rest) == count + 5:
        start, out, held, sems = rest[count + 1 :]
    else:
        start, (out, held, sems) = None, rest[count + 1 :]
    run_all(
        [
            pltpu.make_async_copy(pieces[n], held.at[slots[n]], sems.at[n])
            for n in range(count)
        ]
    )
    per_piece = held.shape[2] // TILE

    def body(tile, carry):
        picked, sets = [], []
        for m in range(links):
            source = sources[tile, m]
            cols = pl.ds(pl.multiple_of(lax.rem(source, per_piece) * TILE, TILE), TILE)
            picked.append(held[lax.div(source, per_piece), :, cols])
            sets.append(table[kinds[tile, m]])
        total = lax.dot_general(
            jnp.concatenate(picked, 1),
            jnp.concatenate(sets, 1),
            (((1,), (1,)), ((), ())),
            preferred_element_type=jnp.float32,
        )
        cols = pl.ds(pl.multiple_of(tile * TILE, TILE), TILE)
        if start is not None:
            total = total + start[:, cols]
        out[:, cols] = total
        return carry

    lax.fori_loop(0, out.shape[1] // TILE, body, 0, unroll=2)


def far(slots, sources, kinds, pieces, table, start, name):
    rows, cols = pieces[0].shape
    tiles, links = sources.shape
    count = len(pieces)
    extra = [] if start is None else [start]
    return pl.pallas_call(
        functools.partial(far_kernel, count, links),
        out_shape=jax.ShapeDtypeStruct((rows, tiles * TILE), jnp.float32),
        in_specs=[SMEM] * 3 + [ANY] * count + [VMEM] * (1 + len(extra)),
        out_specs=VMEM,
        scratch_shapes=[
            pltpu.VMEM((count, rows, cols), pieces[0].dtype),
            pltpu.SemaphoreType.DMA((count,)),
        ],
        cost_estimate=cost(2 * tiles * links * rows * TILE * TILE, 6 * rows * cols * count),
        compiler_params=pltpu.CompilerParams(vmem_limit_bytes=LIMIT),
        name=name,
    )(slots, sources, kinds, *pieces, table, *extra)


def last_kernel(place, start, p0, p1, p2, p3, out):
    width = p0.shape[1]
    for d, piece in enumerate((p0, p1, p2, p3)):
        quarter = lax.rem(place[0] - d + RING, RING)
        cols = pl.ds(pl.multiple_of(quarter * width, width), width)
        out[:, cols] = (start[:, cols] + piece[...].astype(jnp.float32)).astype(out.dtype)


def last(place, start, pieces):
    rows, cols = start.shape
    return pl.pallas_call(
        last_kernel,
        out_shape=jax.ShapeDtypeStruct((rows, cols), pieces[0].dtype),
        in_specs=[SMEM] + [VMEM] * (1 + RING),
        out_specs=VMEM,
        cost_estimate=cost(rows * cols, 8 * rows * cols),
        compiler_params=pltpu.CompilerParams(vmem_limit_bytes=LIMIT),
        name="last",
    )(place, start, *pieces)


def around(value, axis, distance):
    count = lax.axis_size(axis)
    return lax.ppermute(value, axis, [(i, (i + distance) % count) for i in range(count)])


def along(value, axis, distance):
    count = lax.axis_size(axis)
    return lax.ppermute(
        value, axis, [(i, i + distance) for i in range(count) if 0 <= i + distance < count]
    )


def exchanged(pieces):
    return [pieces[0]] + [around(pieces[d], "ring", d) for d in range(1, RING)]


def local(
    coeffs,
    beta_list,
    beta_kind,
    opp_beta_kind,
    alpha_list,
    alpha_kind,
    opp_list,
    opp_kind,
    beta_table,
    alpha_table,
    opp_alpha_table,
    opp_beta_table,
):
    own = coeffs[0]
    spot = lax.axis_index("ring").astype(jnp.int32)
    row = lax.axis_index("row").astype(jnp.int32)
    core = lax.axis_index("beta").astype(jnp.int32)
    place = jnp.stack([spot, row])
    order = jnp.arange(RING, dtype=jnp.int32)
    quarters = lax.rem(spot - order + RING, RING)
    half_slots = jnp.concatenate([core * RING + quarters, (1 - core) * RING + quarters])

    pieces = exchanged(cut(place, own))
    other = around(own, "beta", 1)
    up, down = edges(place, pieces)
    above = along(up, "row", 1)
    below = along(down, "row", -1)
    same = far(
        jnp.stack([core, 1 - core]), beta_list, beta_kind, [own, other], beta_table, None, "same"
    )
    half = exchanged(
        near(place, opp_list, opp_kind, pieces, above, below, opp_alpha_table, "half")
    )
    alpha = exchanged(
        near(place, alpha_list, alpha_kind, pieces, above, below, alpha_table, "alpha")
    )
    half_other = [around(piece, "beta", 1) for piece in half]
    mixed = far(
        half_slots, beta_list, opp_beta_kind, half + half_other, opp_beta_table, same, "mixed"
    )
    return last(place, mixed, alpha)[None]


def solution(mesh):
    split = Mesh(
        mesh.devices.reshape(-1, RING, mesh.devices.shape[1]), ("row", "ring", "beta")
    )
    vector = P(None, ("row", "ring"), "beta")
    lists = P("beta", None)
    placed = (vector, lists, lists, lists) + (P(),) * 8
    return jax.shard_map(
        local, mesh=split, in_specs=placed, out_specs=vector, check_vma=False
    )
```

```python
import functools

import jax
import jax.numpy as jnp
from jax import lax
from jax.experimental import pallas as pl
from jax.experimental.pallas import tpu as pltpu
from jax.sharding import Mesh, PartitionSpec as P

REACH = 3
RING = 4
TILE = 128
SMEM = pl.BlockSpec(memory_space=pltpu.SMEM)
ANY = pl.BlockSpec(memory_space=pl.ANY)
VMEM = pl.BlockSpec(memory_space=pltpu.VMEM)
LIMIT = 10 << 20
MARK = 1 << 20


def cost(flops, moved):
    return pl.CostEstimate(flops=flops, bytes_accessed=moved, transcendentals=0)


def cut_kernel(whole, *pieces):
    spot = lax.axis_index("ring")
    width = whole.shape[1] // RING
    for d in range(RING):
        quarter = lax.bitwise_xor(spot, d)
        cols = pl.ds(pl.multiple_of(quarter * width, width), width)
        pieces[d][...] = whole[:, cols]


def cut(whole):
    rows, cols = whole.shape
    piece = jax.ShapeDtypeStruct((rows, cols // RING), whole.dtype)
    return pl.pallas_call(
        cut_kernel,
        out_shape=[piece] * RING,
        in_specs=[VMEM],
        out_specs=[VMEM] * RING,
        cost_estimate=cost(0, 4 * rows * cols),
        compiler_params=pltpu.CompilerParams(vmem_limit_bytes=LIMIT),
        name="cut",
    )(whole)


def edge_kernel(p0, p1, p2, p3, even, odd):
    spot = lax.axis_index("ring")
    parity = lax.rem(lax.axis_index("row"), 2)
    for d, piece in enumerate((p0, p1, p2, p3)):
        block = lax.bitwise_xor(spot, d)
        for part, shift in ((even, 1 - parity), (odd, parity)):
            at = block - shift

            @pl.when((at >= 0) & (at < REACH))
            def _():
                part[at] = piece[...]


def edges(pieces):
    rows, cols = pieces[0].shape
    part = jax.ShapeDtypeStruct((REACH, rows, cols), pieces[0].dtype)
    return pl.pallas_call(
        edge_kernel,
        out_shape=[part] * 2,
        in_specs=[VMEM] * RING,
        out_specs=[VMEM] * 2,
        cost_estimate=cost(0, 4 * REACH * rows * cols * 2),
        compiler_params=pltpu.CompilerParams(vmem_limit_bytes=LIMIT),
        name="edges",
    )(*pieces)


def near_kernel(links, sources, kinds, p0, p1, p2, p3, even, odd, table, *rest):
    outs, held = rest[:RING], rest[RING]
    spot, row = lax.axis_index("ring"), lax.axis_index("row")
    parity = lax.rem(row, 2)
    for d, piece in enumerate((p0, p1, p2, p3)):
        held[RING + lax.bitwise_xor(spot, d)] = piece[...]
    for part, below in ((even, 1 - parity), (odd, parity)):
        base = below * 2 * RING + (1 - below)
        for n in range(REACH):
            held[base + n] = part[n]
    first = (row - 1) * RING
    for d in range(RING):
        target = lax.bitwise_xor(spot, d)
        tiles = [table[kinds[target, m]] for m in range(links)]
        picked = [held[sources[target, m] - first] for m in range(links)]
        total = jnp.dot(
            jnp.concatenate(tiles, 1),
            jnp.concatenate(picked, 0),
            preferred_element_type=jnp.float32,
        )
        outs[d][...] = total.astype(outs[d].dtype)


def near(sources, kinds, pieces, even, odd, table, name):
    rows, cols = pieces[0].shape
    links = sources.shape[1]
    piece = jax.ShapeDtypeStruct((rows, cols), pieces[0].dtype)
    return pl.pallas_call(
        functools.partial(near_kernel, links),
        out_shape=[piece] * RING,
        in_specs=[SMEM] * 2 + [VMEM] * (RING + 3),
        out_specs=[VMEM] * RING,
        scratch_shapes=[pltpu.VMEM((3 * RING, rows, cols), pieces[0].dtype)],
        cost_estimate=cost(0, rows * cols),
        compiler_params=pltpu.CompilerParams(vmem_limit_bytes=LIMIT),
        name=name,
    )(sources, kinds, *pieces, even, odd, table)


def beta_tile(held, table, sources, kinds, tile, links):
    per_piece = held.shape[2] // TILE
    picked, sets = [], []
    for m in range(links):
        source = sources[tile, m]
        cols = pl.ds(pl.multiple_of(lax.rem(source, per_piece) * TILE, TILE), TILE)
        picked.append(held[lax.div(source, per_piece), :, cols])
        sets.append(table[kinds[tile, m]])
    return jnp.dot(
        jnp.concatenate(picked, 1),
        jnp.concatenate(sets, 0),
        preferred_element_type=jnp.float32,
    )


def same_kernel(links, sources, kinds, own, other, table, opp_table, out, turned, held, flat):
    core = lax.axis_index("beta")
    held[core] = own[...]
    held[1 - core] = other[...]
    for kind in range(table.shape[0]):
        flat[kind] = table[kind].T
        turned[kind] = opp_table[kind].T

    def body(tile, carry):
        cols = pl.ds(pl.multiple_of(tile * TILE, TILE), TILE)
        out[:, cols] = beta_tile(held, flat, sources, kinds, tile, links)
        return carry

    lax.fori_loop(0, out.shape[1] // TILE, body, 0, unroll=4)


def same_part(sources, kinds, own, other, table, opp_table):
    rows, cols = own.shape
    return pl.pallas_call(
        functools.partial(same_kernel, sources.shape[1]),
        out_shape=[
            jax.ShapeDtypeStruct((rows, cols), jnp.float32),
            jax.ShapeDtypeStruct(opp_table.shape, opp_table.dtype),
        ],
        in_specs=[SMEM] * 2 + [VMEM] * 4,
        out_specs=[VMEM] * 2,
        scratch_shapes=[
            pltpu.VMEM((2, rows, cols), own.dtype),
            pltpu.VMEM(table.shape, table.dtype),
        ],
        cost_estimate=cost(0, rows * cols),
        compiler_params=pltpu.CompilerParams(vmem_limit_bytes=LIMIT),
        name="same",
    )(sources, kinds, own, other, table, opp_table)


def mixed_kernel(links, sources, kinds, table, start, mark, *rest):
    half, other, alpha = rest[:RING], rest[RING : 2 * RING], rest[2 * RING : 3 * RING]
    out, held, added = rest[3 * RING :]
    spot, core = lax.axis_index("ring"), lax.axis_index("beta")
    for d in range(RING):
        quarter = lax.bitwise_xor(spot, d)
        held[core * RING + quarter] = half[d][...]
        held[(1 - core) * RING + quarter] = other[d][...]
        added[quarter] = alpha[d][...]
    per_piece = held.shape[2] // TILE

    def body(tile, carry):
        cols = pl.ds(pl.multiple_of(tile * TILE, TILE), TILE)
        part = pl.ds(pl.multiple_of(lax.rem(tile, per_piece) * TILE, TILE), TILE)
        total = beta_tile(held, table, sources, kinds, tile, links) + start[:, cols]
        total = total + added[lax.div(tile, per_piece), :, part].astype(jnp.float32)
        out[:, cols] = total.astype(out.dtype)
        return carry

    lax.fori_loop(0, out.shape[1] // TILE, body, 0, unroll=4)


def mixed_part(sources, kinds, table, start, mark, half, other, alpha):
    rows, cols = start.shape
    kind = half[0].dtype
    return pl.pallas_call(
        functools.partial(mixed_kernel, sources.shape[1]),
        out_shape=jax.ShapeDtypeStruct((rows, cols), kind),
        in_specs=[SMEM] * 2 + [VMEM] * 2 + [ANY] + [VMEM] * (3 * RING),
        out_specs=VMEM,
        scratch_shapes=[
            pltpu.VMEM((2 * RING, rows, cols // RING), kind),
            pltpu.VMEM((RING, rows, cols // RING), kind),
        ],
        cost_estimate=cost(0, rows * cols),
        compiler_params=pltpu.CompilerParams(vmem_limit_bytes=LIMIT),
        name="mixed",
    )(sources, kinds, table, start, mark, *half, *other, *alpha)


def mark_kernel(*refs):
    refs[-1][...] = jnp.zeros_like(refs[-1])


def marked(pieces):
    return pl.pallas_call(
        mark_kernel,
        out_shape=jax.ShapeDtypeStruct((8, TILE), jnp.float32),
        in_specs=[ANY] * len(pieces),
        out_specs=VMEM,
        cost_estimate=cost(0, MARK),
        compiler_params=pltpu.CompilerParams(vmem_limit_bytes=LIMIT),
        name="mark",
    )(*pieces)


def swapped(value, axis, flip):
    return lax.ppermute(value, axis, [(i, i ^ flip) for i in range(lax.axis_size(axis))])


def exchanged(pieces):
    return [pieces[0]] + [swapped(pieces[d], "ring", d) for d in range(1, RING)]


def handed(value, parity):
    count = lax.axis_size("row")
    pairs = [(row, row + 1) for row in range(parity, count - 1, 2)]
    return lax.ppermute(value, "row", pairs + [(there, here) for here, there in pairs])


def local(
    coeffs,
    beta_list,
    beta_kind,
    opp_beta_kind,
    alpha_list,
    alpha_kind,
    opp_list,
    opp_kind,
    beta_table,
    alpha_table,
    opp_alpha_table,
    opp_beta_table,
):
    own = coeffs[0]
    row = lax.axis_index("row")

    def mine(lists):
        return lax.dynamic_slice_in_dim(lists, row * RING, RING, 0)

    pieces = exchanged(cut(own))
    other = swapped(own, "beta", 1)
    same, turned = same_part(
        beta_list, beta_kind, own, other, beta_table, opp_beta_table
    )
    even, odd = edges(pieces)
    even, odd = handed(even, 0), handed(odd, 1)
    even, odd, same = lax.optimization_barrier((even, odd, same))
    half = exchanged(near(mine(opp_list), mine(opp_kind), pieces, even, odd, opp_alpha_table, "half"))
    formed = near(mine(alpha_list), mine(alpha_kind), pieces, even, odd, alpha_table, "alpha")
    half, mark = lax.optimization_barrier((half, formed[0]))
    alpha = exchanged(formed)
    half_other = [swapped(piece, "beta", 1) for piece in half]
    mark = marked(alpha[1:])
    total = mixed_part(
        beta_list, opp_beta_kind, turned, same, mark, half, half_other, alpha
    )
    return total[None]


def solution(mesh):
    split = Mesh(
        mesh.devices.reshape(-1, RING, mesh.devices.shape[1]), ("row", "ring", "beta")
    )
    vector = P(None, ("row", "ring"), "beta")
    lists = P("beta", None)
    placed = (vector, lists, lists, lists) + (P(),) * 8
    return jax.shard_map(
        local, mesh=split, in_specs=placed, out_specs=vector, check_vma=False
    )
```

```python
import functools

import jax
import jax.numpy as jnp
from jax import lax
from jax.experimental import pallas as pl
from jax.experimental.pallas import tpu as pltpu
from jax.sharding import Mesh, PartitionSpec as P

REACH = 3
RING = 4
TILE = 128
SMEM = pl.BlockSpec(memory_space=pltpu.SMEM)
ANY = pl.BlockSpec(memory_space=pl.ANY)
VMEM = pl.BlockSpec(memory_space=pltpu.VMEM)
LIMIT = 10 << 20
MARK = 1 << 20


def cost(flops, moved):
    return pl.CostEstimate(flops=flops, bytes_accessed=moved, transcendentals=0)


def cut_kernel(whole, *pieces):
    spot = lax.axis_index("ring")
    width = whole.shape[1] // RING
    for d in range(RING):
        quarter = lax.bitwise_xor(spot, d)
        cols = pl.ds(pl.multiple_of(quarter * width, width), width)
        pieces[d][...] = whole[:, cols]


def cut(whole):
    rows, cols = whole.shape
    piece = jax.ShapeDtypeStruct((rows, cols // RING), whole.dtype)
    return pl.pallas_call(
        cut_kernel,
        out_shape=[piece] * RING,
        in_specs=[VMEM],
        out_specs=[VMEM] * RING,
        cost_estimate=cost(0, 4 * rows * cols),
        compiler_params=pltpu.CompilerParams(vmem_limit_bytes=LIMIT),
        name="cut",
    )(whole)


def edge_kernel(p0, p1, p3, p2, even, odd):
    spot = lax.axis_index("ring")
    parity = lax.rem(lax.axis_index("row"), 2)
    for d, piece in enumerate((p0, p1, p2, p3)):
        block = lax.bitwise_xor(spot, d)
        for part, shift in ((even, 1 - parity), (odd, parity)):
            at = block - shift

            @pl.when((at >= 0) & (at < REACH))
            def _():
                part[at] = piece[...]


def edges(pieces):
    rows, cols = pieces[0].shape
    part = jax.ShapeDtypeStruct((REACH, rows, cols), pieces[0].dtype)
    return pl.pallas_call(
        edge_kernel,
        out_shape=[part] * 2,
        in_specs=[VMEM] * RING,
        out_specs=[VMEM] * 2,
        cost_estimate=cost(0, 4 * REACH * rows * cols * 2),
        compiler_params=pltpu.CompilerParams(vmem_limit_bytes=LIMIT),
        name="edges",
    )(*[pieces[d] for d in (0, 1, 3, 2)])


def near_kernel(links, sources, kinds, p0, p1, p2, p3, even, odd, table, *rest):
    outs, held = rest[:RING], rest[RING]
    spot, row = lax.axis_index("ring"), lax.axis_index("row")
    parity = lax.rem(row, 2)
    for d, piece in enumerate((p0, p1, p2, p3)):
        held[RING + lax.bitwise_xor(spot, d)] = piece[...]
    for part, below in ((even, 1 - parity), (odd, parity)):
        base = below * 2 * RING + (1 - below)
        for n in range(REACH):
            held[base + n] = part[n]
    first = (row - 1) * RING
    for d in range(RING):
        target = lax.bitwise_xor(spot, d)
        tiles = [table[kinds[target, m]] for m in range(links)]
        picked = [held[sources[target, m] - first] for m in range(links)]
        total = jnp.dot(
            jnp.concatenate(tiles, 1),
            jnp.concatenate(picked, 0),
            preferred_element_type=jnp.float32,
        )
        outs[d][...] = total.astype(outs[d].dtype)


def near(sources, kinds, pieces, even, odd, table, name):
    rows, cols = pieces[0].shape
    links = sources.shape[1]
    piece = jax.ShapeDtypeStruct((rows, cols), pieces[0].dtype)
    return pl.pallas_call(
        functools.partial(near_kernel, links),
        out_shape=[piece] * RING,
        in_specs=[SMEM] * 2 + [VMEM] * (RING + 3),
        out_specs=[VMEM] * RING,
        scratch_shapes=[pltpu.VMEM((3 * RING, rows, cols), pieces[0].dtype)],
        cost_estimate=cost(0, rows * cols),
        compiler_params=pltpu.CompilerParams(vmem_limit_bytes=LIMIT),
        name=name,
    )(sources, kinds, *pieces, even, odd, table)


def beta_tile(held, table, sources, kinds, tile, links):
    per_piece = held.shape[2] // TILE
    picked, sets = [], []
    for m in range(links):
        source = sources[tile, m]
        cols = pl.ds(pl.multiple_of(lax.rem(source, per_piece) * TILE, TILE), TILE)
        picked.append(held[lax.div(source, per_piece), :, cols])
        sets.append(table[kinds[tile, m]])
    return jnp.dot(
        jnp.concatenate(picked, 1),
        jnp.concatenate(sets, 0),
        preferred_element_type=jnp.float32,
    )


def same_kernel(links, sources, kinds, own, other, table, opp_table, out, turned, held, flat):
    core = lax.axis_index("beta")
    held[core] = own[...]
    held[1 - core] = other[...]
    for kind in range(table.shape[0]):
        flat[kind] = table[kind].T
        turned[kind] = opp_table[kind].T

    def body(tile, carry):
        cols = pl.ds(pl.multiple_of(tile * TILE, TILE), TILE)
        out[:, cols] = beta_tile(held, flat, sources, kinds, tile, links)
        return carry

    lax.fori_loop(0, out.shape[1] // TILE, body, 0, unroll=4)


def same_part(sources, kinds, own, other, table, opp_table):
    rows, cols = own.shape
    return pl.pallas_call(
        functools.partial(same_kernel, sources.shape[1]),
        out_shape=[
            jax.ShapeDtypeStruct((rows, cols), jnp.float32),
            jax.ShapeDtypeStruct(opp_table.shape, opp_table.dtype),
        ],
        in_specs=[SMEM] * 2 + [VMEM] * 4,
        out_specs=[VMEM] * 2,
        scratch_shapes=[
            pltpu.VMEM((2, rows, cols), own.dtype),
            pltpu.VMEM(table.shape, table.dtype),
        ],
        cost_estimate=cost(0, rows * cols),
        compiler_params=pltpu.CompilerParams(vmem_limit_bytes=LIMIT),
        name="same",
    )(sources, kinds, own, other, table, opp_table)


def mixed_kernel(links, sources, kinds, table, start, mark, *rest):
    half, other, alpha = rest[:RING], rest[RING : 2 * RING], rest[2 * RING : 3 * RING]
    out, held, added = rest[3 * RING :]
    spot, core = lax.axis_index("ring"), lax.axis_index("beta")
    for d in range(RING):
        quarter = lax.bitwise_xor(spot, d)
        held[core * RING + quarter] = half[d][...]
        held[(1 - core) * RING + quarter] = other[d][...]
        added[quarter] = alpha[d][...]
    per_piece = held.shape[2] // TILE

    def body(tile, carry):
        cols = pl.ds(pl.multiple_of(tile * TILE, TILE), TILE)
        part = pl.ds(pl.multiple_of(lax.rem(tile, per_piece) * TILE, TILE), TILE)
        total = beta_tile(held, table, sources, kinds, tile, links) + start[:, cols]
        total = total + added[lax.div(tile, per_piece), :, part].astype(jnp.float32)
        out[:, cols] = total.astype(out.dtype)
        return carry

    lax.fori_loop(0, out.shape[1] // TILE, body, 0, unroll=4)


def mixed_part(sources, kinds, table, start, mark, half, other, alpha):
    rows, cols = start.shape
    kind = half[0].dtype
    return pl.pallas_call(
        functools.partial(mixed_kernel, sources.shape[1]),
        out_shape=jax.ShapeDtypeStruct((rows, cols), kind),
        in_specs=[SMEM] * 2 + [VMEM] * 2 + [ANY] + [VMEM] * (3 * RING),
        out_specs=VMEM,
        scratch_shapes=[
            pltpu.VMEM((2 * RING, rows, cols // RING), kind),
            pltpu.VMEM((RING, rows, cols // RING), kind),
        ],
        cost_estimate=cost(0, rows * cols),
        compiler_params=pltpu.CompilerParams(vmem_limit_bytes=LIMIT),
        name="mixed",
    )(sources, kinds, table, start, mark, *half, *other, *alpha)


def mark_kernel(*refs):
    refs[-1][...] = jnp.zeros_like(refs[-1])


def marked(pieces):
    return pl.pallas_call(
        mark_kernel,
        out_shape=jax.ShapeDtypeStruct((8, TILE), jnp.float32),
        in_specs=[ANY] * len(pieces),
        out_specs=VMEM,
        cost_estimate=cost(0, MARK),
        compiler_params=pltpu.CompilerParams(vmem_limit_bytes=LIMIT),
        name="mark",
    )(*pieces)


def swapped(value, axis, flip):
    return lax.ppermute(value, axis, [(i, i ^ flip) for i in range(lax.axis_size(axis))])


def exchanged(pieces):
    return [pieces[0]] + [swapped(pieces[d], "ring", d) for d in range(1, RING)]


def handed(value, parity):
    count = lax.axis_size("row")
    pairs = [(row, row + 1) for row in range(parity, count - 1, 2)]
    return lax.ppermute(value, "row", pairs + [(there, here) for here, there in pairs])


def local(
    coeffs,
    beta_list,
    beta_kind,
    opp_beta_kind,
    alpha_list,
    alpha_kind,
    opp_list,
    opp_kind,
    beta_table,
    alpha_table,
    opp_alpha_table,
    opp_beta_table,
):
    own = coeffs[0]
    row = lax.axis_index("row")

    def mine(lists):
        return lax.dynamic_slice_in_dim(lists, row * RING, RING, 0)

    pieces = exchanged(cut(own))
    other = swapped(own, "beta", 1)
    same, turned = same_part(
        beta_list, beta_kind, own, other, beta_table, opp_beta_table
    )
    even, odd = edges(pieces)
    even, odd = handed(even, 0), handed(odd, 1)
    even, odd, same = lax.optimization_barrier((even, odd, same))
    half = exchanged(near(mine(opp_list), mine(opp_kind), pieces, even, odd, opp_alpha_table, "half"))
    formed = near(mine(alpha_list), mine(alpha_kind), pieces, even, odd, alpha_table, "alpha")
    half = [half[d] for d in (0, 2, 1, 3)]
    half, mark = lax.optimization_barrier((half, formed[0]))
    half = [half[d] for d in (0, 2, 1, 3)]
    alpha = exchanged(formed)
    half_other = [swapped(piece, "beta", 1) for piece in half]
    mark = marked([alpha[d] for d in (1, 3, 2)])
    total = mixed_part(
        beta_list, opp_beta_kind, turned, same, mark, half, half_other, alpha
    )
    return total[None]


def solution(mesh):
    split = Mesh(
        mesh.devices.reshape(-1, RING, mesh.devices.shape[1]), ("row", "ring", "beta")
    )
    vector = P(None, ("row", "ring"), "beta")
    lists = P("beta", None)
    placed = (vector, lists, lists, lists) + (P(),) * 8
    return jax.shard_map(
        local, mesh=split, in_specs=placed, out_specs=vector, check_vma=False
    )
```

```python
import functools

import jax
import jax.numpy as jnp
from jax import lax
from jax.experimental import pallas as pl
from jax.experimental.pallas import tpu as pltpu
from jax.sharding import Mesh, PartitionSpec as P

REACH = 3
RING = 4
TILE = 128
SMEM = pl.BlockSpec(memory_space=pltpu.SMEM)
ANY = pl.BlockSpec(memory_space=pl.ANY)
VMEM = pl.BlockSpec(memory_space=pltpu.VMEM)
LIMIT = 10 << 20
MARK = 1 << 20


def cost(flops, moved):
    return pl.CostEstimate(flops=flops, bytes_accessed=moved, transcendentals=0)


def cut_kernel(whole, *pieces):
    spot = lax.axis_index("ring")
    width = whole.shape[1] // RING
    for d in range(RING):
        quarter = lax.bitwise_xor(spot, d)
        cols = pl.ds(pl.multiple_of(quarter * width, width), width)
        pieces[d][...] = whole[:, cols]


def cut(whole):
    rows, cols = whole.shape
    piece = jax.ShapeDtypeStruct((rows, cols // RING), whole.dtype)
    return pl.pallas_call(
        cut_kernel,
        out_shape=[piece] * RING,
        in_specs=[VMEM],
        out_specs=[VMEM] * RING,
        cost_estimate=cost(0, 4 * rows * cols),
        compiler_params=pltpu.CompilerParams(vmem_limit_bytes=LIMIT),
        name="cut",
    )(whole)


def edge_kernel(p0, p1, p3, p2, even, odd):
    spot = lax.axis_index("ring")
    parity = lax.rem(lax.axis_index("row"), 2)
    for d, piece in enumerate((p0, p1, p2, p3)):
        block = lax.bitwise_xor(spot, d)
        for part, shift in ((even, 1 - parity), (odd, parity)):
            at = block - shift

            @pl.when((at >= 0) & (at < REACH))
            def _():
                part[at] = piece[...]


def edges(pieces):
    rows, cols = pieces[0].shape
    part = jax.ShapeDtypeStruct((REACH, rows, cols), pieces[0].dtype)
    return pl.pallas_call(
        edge_kernel,
        out_shape=[part] * 2,
        in_specs=[VMEM] * RING,
        out_specs=[VMEM] * 2,
        cost_estimate=cost(0, 4 * REACH * rows * cols * 2),
        compiler_params=pltpu.CompilerParams(vmem_limit_bytes=LIMIT),
        name="edges",
    )(*[pieces[d] for d in (0, 1, 3, 2)])


def near_kernel(links, sources, kinds, p0, p1, p2, p3, even, odd, table, *rest):
    outs, held = rest[:RING], rest[RING]
    spot, row = lax.axis_index("ring"), lax.axis_index("row")
    parity = lax.rem(row, 2)
    for d, piece in enumerate((p0, p1, p2, p3)):
        held[RING + lax.bitwise_xor(spot, d)] = piece[...]
    for part, below in ((even, 1 - parity), (odd, parity)):
        base = below * 2 * RING + (1 - below)
        for n in range(REACH):
            held[base + n] = part[n]
    first = (row - 1) * RING
    for d in range(RING):
        target = lax.bitwise_xor(spot, d)
        tiles = [table[kinds[target, m]] for m in range(links)]
        picked = [held[sources[target, m] - first] for m in range(links)]
        total = jnp.dot(
            jnp.concatenate(tiles, 1),
            jnp.concatenate(picked, 0),
            preferred_element_type=jnp.float32,
        )
        outs[d][...] = total.astype(outs[d].dtype)


def near(sources, kinds, pieces, even, odd, table, name):
    rows, cols = pieces[0].shape
    links = sources.shape[1]
    piece = jax.ShapeDtypeStruct((rows, cols), pieces[0].dtype)
    return pl.pallas_call(
        functools.partial(near_kernel, links),
        out_shape=[piece] * RING,
        in_specs=[SMEM] * 2 + [VMEM] * (RING + 3),
        out_specs=[VMEM] * RING,
        scratch_shapes=[pltpu.VMEM((3 * RING, rows, cols), pieces[0].dtype)],
        cost_estimate=cost(0, rows * cols),
        compiler_params=pltpu.CompilerParams(vmem_limit_bytes=LIMIT),
        name=name,
    )(sources, kinds, *pieces, even, odd, table)


def beta_tile(held, table, sources, kinds, tile, links):
    per_piece = held.shape[2] // TILE
    picked, sets = [], []
    for m in range(links):
        source = sources[tile, m]
        cols = pl.ds(pl.multiple_of(lax.rem(source, per_piece) * TILE, TILE), TILE)
        picked.append(held[lax.div(source, per_piece), :, cols])
        sets.append(table[kinds[tile, m]])
    return jnp.dot(
        jnp.concatenate(picked, 1),
        jnp.concatenate(sets, 0),
        preferred_element_type=jnp.float32,
    )


def same_kernel(links, sources, kinds, own, other, table, opp_table, out, turned, held, flat):
    core = lax.axis_index("beta")
    held[core] = own[...]
    held[1 - core] = other[...]
    for kind in range(table.shape[0]):
        flat[kind] = table[kind].T
        turned[kind] = opp_table[kind].T

    def body(tile, carry):
        cols = pl.ds(pl.multiple_of(tile * TILE, TILE), TILE)
        out[:, cols] = beta_tile(held, flat, sources, kinds, tile, links)
        return carry

    lax.fori_loop(0, out.shape[1] // TILE, body, 0, unroll=16)


def same_part(sources, kinds, own, other, table, opp_table):
    rows, cols = own.shape
    return pl.pallas_call(
        functools.partial(same_kernel, sources.shape[1]),
        out_shape=[
            jax.ShapeDtypeStruct((rows, cols), jnp.float32),
            jax.ShapeDtypeStruct(opp_table.shape, opp_table.dtype),
        ],
        in_specs=[SMEM] * 2 + [VMEM] * 4,
        out_specs=[VMEM] * 2,
        scratch_shapes=[
            pltpu.VMEM((2, rows, cols), own.dtype),
            pltpu.VMEM(table.shape, table.dtype),
        ],
        cost_estimate=cost(0, rows * cols),
        compiler_params=pltpu.CompilerParams(vmem_limit_bytes=LIMIT),
        name="same",
    )(sources, kinds, own, other, table, opp_table)


def mixed_kernel(links, sources, kinds, table, start, mark, *rest):
    half, other, alpha = rest[:RING], rest[RING : 2 * RING], rest[2 * RING : 3 * RING]
    out, held, added = rest[3 * RING :]
    spot, core = lax.axis_index("ring"), lax.axis_index("beta")
    for d in range(RING):
        quarter = lax.bitwise_xor(spot, d)
        held[core * RING + quarter] = half[d][...]
        held[(1 - core) * RING + quarter] = other[d][...]
        added[quarter] = alpha[d][...]
    per_piece = held.shape[2] // TILE

    def body(tile, carry):
        cols = pl.ds(pl.multiple_of(tile * TILE, TILE), TILE)
        part = pl.ds(pl.multiple_of(lax.rem(tile, per_piece) * TILE, TILE), TILE)
        total = beta_tile(held, table, sources, kinds, tile, links) + start[:, cols]
        total = total + added[lax.div(tile, per_piece), :, part].astype(jnp.float32)
        out[:, cols] = total.astype(out.dtype)
        return carry

    lax.fori_loop(0, out.shape[1] // TILE, body, 0, unroll=16)


def mixed_part(sources, kinds, table, start, mark, half, other, alpha):
    rows, cols = start.shape
    kind = half[0].dtype
    return pl.pallas_call(
        functools.partial(mixed_kernel, sources.shape[1]),
        out_shape=jax.ShapeDtypeStruct((rows, cols), kind),
        in_specs=[SMEM] * 2 + [VMEM] * 2 + [ANY] + [VMEM] * (3 * RING),
        out_specs=VMEM,
        scratch_shapes=[
            pltpu.VMEM((2 * RING, rows, cols // RING), kind),
            pltpu.VMEM((RING, rows, cols // RING), kind),
        ],
        cost_estimate=cost(0, rows * cols),
        compiler_params=pltpu.CompilerParams(vmem_limit_bytes=LIMIT),
        name="mixed",
    )(sources, kinds, table, start, mark, *half, *other, *alpha)


def mark_kernel(*refs):
    refs[-1][...] = jnp.zeros_like(refs[-1])


def marked(pieces):
    return pl.pallas_call(
        mark_kernel,
        out_shape=jax.ShapeDtypeStruct((8, TILE), jnp.float32),
        in_specs=[ANY] * len(pieces),
        out_specs=VMEM,
        cost_estimate=cost(0, MARK),
        compiler_params=pltpu.CompilerParams(vmem_limit_bytes=LIMIT),
        name="mark",
    )(*pieces)


def swapped(value, axis, flip):
    return lax.ppermute(value, axis, [(i, i ^ flip) for i in range(lax.axis_size(axis))])


def exchanged(pieces):
    return [pieces[0]] + [swapped(pieces[d], "ring", d) for d in range(1, RING)]


def handed(value, parity):
    count = lax.axis_size("row")
    pairs = [(row, row + 1) for row in range(parity, count - 1, 2)]
    return lax.ppermute(value, "row", pairs + [(there, here) for here, there in pairs])


def local(
    coeffs,
    beta_list,
    beta_kind,
    opp_beta_kind,
    alpha_list,
    alpha_kind,
    opp_list,
    opp_kind,
    beta_table,
    alpha_table,
    opp_alpha_table,
    opp_beta_table,
):
    own = coeffs[0]
    row = lax.axis_index("row")

    def mine(lists):
        return lax.dynamic_slice_in_dim(lists, row * RING, RING, 0)

    pieces = exchanged(cut(own))
    other = swapped(own, "beta", 1)
    same, turned = same_part(
        beta_list, beta_kind, own, other, beta_table, opp_beta_table
    )
    even, odd = edges(pieces)
    even, odd = handed(even, 0), handed(odd, 1)
    even, odd, same = lax.optimization_barrier((even, odd, same))
    half = exchanged(near(mine(opp_list), mine(opp_kind), pieces, even, odd, opp_alpha_table, "half"))
    formed = near(mine(alpha_list), mine(alpha_kind), pieces, even, odd, alpha_table, "alpha")
    half = [half[d] for d in (0, 2, 1, 3)]
    half, mark = lax.optimization_barrier((half, formed[0]))
    half = [half[d] for d in (0, 2, 1, 3)]
    alpha = exchanged(formed)
    half_other = [swapped(piece, "beta", 1) for piece in half]
    mark = marked([alpha[d] for d in (1, 3, 2)])
    total = mixed_part(
        beta_list, opp_beta_kind, turned, same, mark, half, half_other, alpha
    )
    return total[None]


def solution(mesh):
    split = Mesh(
        mesh.devices.reshape(-1, RING, mesh.devices.shape[1]), ("row", "ring", "beta")
    )
    vector = P(None, ("row", "ring"), "beta")
    lists = P("beta", None)
    placed = (vector, lists, lists, lists) + (P(),) * 8
    return jax.shard_map(
        local, mesh=split, in_specs=placed, out_specs=vector, check_vma=False
    )
```

```python
import functools

import jax
import jax.numpy as jnp
from jax import lax
from jax.experimental import pallas as pl
from jax.experimental.pallas import tpu as pltpu
from jax.sharding import Mesh, PartitionSpec as P

REACH = 3
RING = 4
TILE = 128
SMEM = pl.BlockSpec(memory_space=pltpu.SMEM)
ANY = pl.BlockSpec(memory_space=pl.ANY)
VMEM = pl.BlockSpec(memory_space=pltpu.VMEM)
LIMIT = 10 << 20
MARK = 1 << 20


def cost(flops, moved):
    return pl.CostEstimate(flops=flops, bytes_accessed=moved, transcendentals=0)


def cut_kernel(whole, *pieces):
    spot = lax.axis_index("ring")
    width = whole.shape[1] // RING
    for d in range(RING):
        quarter = lax.bitwise_xor(spot, d)
        cols = pl.ds(pl.multiple_of(quarter * width, width), width)
        pieces[d][...] = whole[:, cols]


def cut(whole):
    rows, cols = whole.shape
    piece = jax.ShapeDtypeStruct((rows, cols // RING), whole.dtype)
    return pl.pallas_call(
        cut_kernel,
        out_shape=[piece] * RING,
        in_specs=[VMEM],
        out_specs=[VMEM] * RING,
        cost_estimate=cost(0, 4 * rows * cols),
        compiler_params=pltpu.CompilerParams(vmem_limit_bytes=LIMIT),
        name="cut",
    )(whole)


def edge_kernel(p0, p1, p3, p2, even, odd):
    spot = lax.axis_index("ring")
    parity = lax.rem(lax.axis_index("row"), 2)
    for d, piece in enumerate((p0, p1, p2, p3)):
        block = lax.bitwise_xor(spot, d)
        for part, shift in ((even, 1 - parity), (odd, parity)):
            at = block - shift

            @pl.when((at >= 0) & (at < REACH))
            def _():
                part[at] = piece[...]


def edges(pieces):
    rows, cols = pieces[0].shape
    part = jax.ShapeDtypeStruct((REACH, rows, cols), pieces[0].dtype)
    return pl.pallas_call(
        edge_kernel,
        out_shape=[part] * 2,
        in_specs=[VMEM] * RING,
        out_specs=[VMEM] * 2,
        cost_estimate=cost(0, 4 * REACH * rows * cols * 2),
        compiler_params=pltpu.CompilerParams(vmem_limit_bytes=LIMIT),
        name="edges",
    )(*[pieces[d] for d in (0, 1, 3, 2)])


def near_kernel(links, sources, kinds, p0, p1, p2, p3, even, odd, table, *rest):
    outs, held = rest[:RING], rest[RING]
    spot, row = lax.axis_index("ring"), lax.axis_index("row")
    parity = lax.rem(row, 2)
    for d, piece in enumerate((p0, p1, p2, p3)):
        held[RING + lax.bitwise_xor(spot, d)] = piece[...]
    for part, below in ((even, 1 - parity), (odd, parity)):
        base = below * 2 * RING + (1 - below)
        for n in range(REACH):
            held[base + n] = part[n]
    first = (row - 1) * RING
    for d in range(RING):
        target = lax.bitwise_xor(spot, d)
        tiles = [table[kinds[target, m]] for m in range(links)]
        picked = [held[sources[target, m] - first] for m in range(links)]
        total = jnp.dot(
            jnp.concatenate(tiles, 1),
            jnp.concatenate(picked, 0),
            preferred_element_type=jnp.float32,
        )
        outs[d][...] = total.astype(outs[d].dtype)


def near(sources, kinds, pieces, even, odd, table, name):
    rows, cols = pieces[0].shape
    links = sources.shape[1]
    piece = jax.ShapeDtypeStruct((rows, cols), pieces[0].dtype)
    return pl.pallas_call(
        functools.partial(near_kernel, links),
        out_shape=[piece] * RING,
        in_specs=[SMEM] * 2 + [VMEM] * (RING + 3),
        out_specs=[VMEM] * RING,
        scratch_shapes=[pltpu.VMEM((3 * RING, rows, cols), pieces[0].dtype)],
        cost_estimate=cost(0, rows * cols),
        compiler_params=pltpu.CompilerParams(vmem_limit_bytes=LIMIT),
        name=name,
    )(sources, kinds, *pieces, even, odd, table)


def beta_tile(held, table, sources, kinds, tile, links):
    per_piece = held.shape[2] // TILE
    picked, sets = [], []
    for m in range(links):
        source = sources[tile, m]
        cols = pl.ds(pl.multiple_of(lax.rem(source, per_piece) * TILE, TILE), TILE)
        picked.append(held[lax.div(source, per_piece), :, cols])
        sets.append(table[kinds[tile, m]])
    return jnp.dot(
        jnp.concatenate(picked, 1),
        jnp.concatenate(sets, 0),
        preferred_element_type=jnp.float32,
    )


def same_kernel(links, sources, kinds, own, other, table, opp_table, out, turned, held, flat):
    core = lax.axis_index("beta")
    held[core] = own[...]
    held[1 - core] = other[...]
    for kind in range(table.shape[0]):
        flat[kind] = table[kind].T
        turned[kind] = opp_table[kind].T

    def body(tile, carry):
        cols = pl.ds(pl.multiple_of(tile * TILE, TILE), TILE)
        out[:, cols] = beta_tile(held, flat, sources, kinds, tile, links)
        return carry

    lax.fori_loop(0, out.shape[1] // TILE, body, 0, unroll=16)


def same_part(sources, kinds, own, other, table, opp_table):
    rows, cols = own.shape
    return pl.pallas_call(
        functools.partial(same_kernel, sources.shape[1]),
        out_shape=[
            jax.ShapeDtypeStruct((rows, cols), jnp.float32),
            jax.ShapeDtypeStruct(opp_table.shape, opp_table.dtype),
        ],
        in_specs=[SMEM] * 2 + [VMEM] * 4,
        out_specs=[VMEM] * 2,
        scratch_shapes=[
            pltpu.VMEM((2, rows, cols), own.dtype),
            pltpu.VMEM(table.shape, table.dtype),
        ],
        cost_estimate=cost(0, rows * cols),
        compiler_params=pltpu.CompilerParams(vmem_limit_bytes=LIMIT),
        name="same",
    )(sources, kinds, own, other, table, opp_table)


def mixed_kernel(links, sources, kinds, table, start, mark, *rest):
    half, other, alpha = rest[:RING], rest[RING : 2 * RING], rest[2 * RING : 3 * RING]
    out, held, added = rest[3 * RING :]
    spot, core = lax.axis_index("ring"), lax.axis_index("beta")
    for d in range(RING):
        quarter = lax.bitwise_xor(spot, d)
        held[core * RING + quarter] = half[d][...]
        held[(1 - core) * RING + quarter] = other[d][...]
        added[quarter] = alpha[d][...]
    per_piece = held.shape[2] // TILE

    def body(tile, carry):
        cols = pl.ds(pl.multiple_of(tile * TILE, TILE), TILE)
        part = pl.ds(pl.multiple_of(lax.rem(tile, per_piece) * TILE, TILE), TILE)
        total = beta_tile(held, table, sources, kinds, tile, links) + start[:, cols]
        total = total + added[lax.div(tile, per_piece), :, part].astype(jnp.float32)
        out[:, cols] = total.astype(out.dtype)
        return carry

    lax.fori_loop(0, out.shape[1] // TILE, body, 0, unroll=16)


def mixed_part(sources, kinds, table, start, mark, half, other, alpha):
    rows, cols = start.shape
    kind = half[0].dtype
    return pl.pallas_call(
        functools.partial(mixed_kernel, sources.shape[1]),
        out_shape=jax.ShapeDtypeStruct((rows, cols), kind),
        in_specs=[SMEM] * 2 + [VMEM] * 2 + [ANY] + [VMEM] * (3 * RING),
        out_specs=VMEM,
        scratch_shapes=[
            pltpu.VMEM((2 * RING, rows, cols // RING), kind),
            pltpu.VMEM((RING, rows, cols // RING), kind),
        ],
        cost_estimate=cost(0, rows * cols),
        compiler_params=pltpu.CompilerParams(vmem_limit_bytes=LIMIT),
        name="mixed",
    )(sources, kinds, table, start, mark, *half, *other, *alpha)


def mark_kernel(*refs):
    refs[-1][...] = jnp.zeros_like(refs[-1])


def marked(pieces):
    return pl.pallas_call(
        mark_kernel,
        out_shape=jax.ShapeDtypeStruct((8, TILE), jnp.float32),
        in_specs=[ANY] * len(pieces),
        out_specs=VMEM,
        cost_estimate=cost(0, MARK),
        compiler_params=pltpu.CompilerParams(vmem_limit_bytes=LIMIT),
        name="mark",
    )(*pieces)


def swapped(value, axis, flip):
    return lax.ppermute(value, axis, [(i, i ^ flip) for i in range(lax.axis_size(axis))])


def exchanged(pieces):
    return [pieces[0]] + [swapped(pieces[d], "ring", d) for d in range(1, RING)]


def handed(value, parity):
    count = lax.axis_size("row")
    pairs = [(row, row + 1) for row in range(parity, count - 1, 2)]
    return lax.ppermute(value, "row", pairs + [(there, here) for here, there in pairs])


def local(
    coeffs,
    beta_list,
    beta_kind,
    opp_beta_kind,
    alpha_list,
    alpha_kind,
    opp_list,
    opp_kind,
    beta_table,
    alpha_table,
    opp_alpha_table,
    opp_beta_table,
):
    own = coeffs[0]
    row = lax.axis_index("row")

    def mine(lists):
        return lax.dynamic_slice_in_dim(lists, row * RING, RING, 0)

    near_lists = [mine(part) for part in (opp_list, opp_kind, alpha_list, alpha_kind)]
    pieces = exchanged(cut(own))
    other = swapped(own, "beta", 1)
    same, turned = same_part(
        beta_list, beta_kind, own, other, beta_table, opp_beta_table
    )
    even, odd = edges(pieces)
    even, odd = handed(even, 0), handed(odd, 1)
    even, odd, same, near_lists = lax.optimization_barrier((even, odd, same, near_lists))
    half = exchanged(near(*near_lists[:2], pieces, even, odd, opp_alpha_table, "half"))
    formed = near(*near_lists[2:], pieces, even, odd, alpha_table, "alpha")
    half = [half[d] for d in (0, 2, 1, 3)]
    half, mark = lax.optimization_barrier((half, formed[0]))
    half = [half[d] for d in (0, 2, 1, 3)]
    alpha = exchanged(formed)
    half_other = [swapped(piece, "beta", 1) for piece in half]
    mark = marked([alpha[d] for d in (1, 3, 2)])
    total = mixed_part(
        beta_list, opp_beta_kind, turned, same, mark, half, half_other, alpha
    )
    return total[None]


def solution(mesh):
    split = Mesh(
        mesh.devices.reshape(-1, RING, mesh.devices.shape[1]), ("row", "ring", "beta")
    )
    vector = P(None, ("row", "ring"), "beta")
    lists = P("beta", None)
    placed = (vector, lists, lists, lists) + (P(),) * 8
    return jax.shard_map(
        local, mesh=split, in_specs=placed, out_specs=vector, check_vma=False
    )
```

```python
import functools

import jax
import jax.numpy as jnp
from jax import lax
from jax.experimental import pallas as pl
from jax.experimental.pallas import tpu as pltpu
from jax.sharding import Mesh, PartitionSpec as P

REACH = 3
RING = 4
TILE = 128
SMEM = pl.BlockSpec(memory_space=pltpu.SMEM)
ANY = pl.BlockSpec(memory_space=pl.ANY)
VMEM = pl.BlockSpec(memory_space=pltpu.VMEM)
LIMIT = 10 << 20
MARK = 1 << 20


def cost(flops, moved):
    return pl.CostEstimate(flops=flops, bytes_accessed=moved, transcendentals=0)


def cut_kernel(whole, *rest):
    pieces, sems = rest[:RING], rest[RING]
    spot = lax.axis_index("ring")
    width = whole.shape[1] // RING
    copies = []
    for d in range(RING):
        quarter = lax.bitwise_xor(spot, d)
        cols = pl.ds(pl.multiple_of(quarter * width, width), width)
        copies.append(pltpu.make_async_copy(whole.at[:, cols], pieces[d], sems.at[d]))
    for copy in copies:
        copy.start()
    for copy in copies:
        copy.wait()


def cut(whole):
    rows, cols = whole.shape
    piece = jax.ShapeDtypeStruct((rows, cols // RING), whole.dtype)
    return pl.pallas_call(
        cut_kernel,
        out_shape=[piece] * RING,
        in_specs=[ANY],
        out_specs=[VMEM] * RING,
        scratch_shapes=[pltpu.SemaphoreType.DMA((RING,))],
        cost_estimate=cost(0, 4 * rows * cols),
        compiler_params=pltpu.CompilerParams(vmem_limit_bytes=LIMIT),
        name="cut",
    )(whole)


def edge_kernel(p0, p1, p3, p2, even, odd):
    spot = lax.axis_index("ring")
    parity = lax.rem(lax.axis_index("row"), 2)
    for d, piece in enumerate((p0, p1, p2, p3)):
        block = lax.bitwise_xor(spot, d)
        for part, shift in ((even, 1 - parity), (odd, parity)):
            at = block - shift

            @pl.when((at >= 0) & (at < REACH))
            def _():
                part[at] = piece[...]


def edges(pieces):
    rows, cols = pieces[0].shape
    part = jax.ShapeDtypeStruct((REACH, rows, cols), pieces[0].dtype)
    return pl.pallas_call(
        edge_kernel,
        out_shape=[part] * 2,
        in_specs=[VMEM] * RING,
        out_specs=[VMEM] * 2,
        cost_estimate=cost(0, 4 * REACH * rows * cols * 2),
        compiler_params=pltpu.CompilerParams(vmem_limit_bytes=LIMIT),
        name="edges",
    )(*[pieces[d] for d in (0, 1, 3, 2)])


def near_kernel(links, sources, kinds, p0, p1, p2, p3, even, odd, table, *rest):
    outs, held = rest[:RING], rest[RING]
    spot, row = lax.axis_index("ring"), lax.axis_index("row")
    parity = lax.rem(row, 2)
    for d, piece in enumerate((p0, p1, p2, p3)):
        held[RING + lax.bitwise_xor(spot, d)] = piece[...]
    for part, below in ((even, 1 - parity), (odd, parity)):
        base = below * 2 * RING + (1 - below)
        for n in range(REACH):
            held[base + n] = part[n]
    first = (row - 1) * RING
    for d in range(RING):
        target = lax.bitwise_xor(spot, d)
        tiles = [table[kinds[target, m]] for m in range(links)]
        picked = [held[sources[target, m] - first] for m in range(links)]
        total = jnp.dot(
            jnp.concatenate(tiles, 1),
            jnp.concatenate(picked, 0),
            preferred_element_type=jnp.float32,
        )
        outs[d][...] = total.astype(outs[d].dtype)


def near(sources, kinds, pieces, even, odd, table, name):
    rows, cols = pieces[0].shape
    links = sources.shape[1]
    piece = jax.ShapeDtypeStruct((rows, cols), pieces[0].dtype)
    return pl.pallas_call(
        functools.partial(near_kernel, links),
        out_shape=[piece] * RING,
        in_specs=[SMEM] * 2 + [VMEM] * (RING + 3),
        out_specs=[VMEM] * RING,
        scratch_shapes=[pltpu.VMEM((3 * RING, rows, cols), pieces[0].dtype)],
        cost_estimate=cost(0, rows * cols),
        compiler_params=pltpu.CompilerParams(vmem_limit_bytes=LIMIT),
        name=name,
    )(sources, kinds, *pieces, even, odd, table)


def beta_tile(held, table, sources, kinds, tile, links):
    per_piece = held.shape[2] // TILE
    picked, sets = [], []
    for m in range(links):
        source = sources[tile, m]
        cols = pl.ds(pl.multiple_of(lax.rem(source, per_piece) * TILE, TILE), TILE)
        picked.append(held[lax.div(source, per_piece), :, cols])
        sets.append(table[kinds[tile, m]])
    return jnp.dot(
        jnp.concatenate(picked, 1),
        jnp.concatenate(sets, 0),
        preferred_element_type=jnp.float32,
    )


def same_kernel(links, sources, kinds, own, other, table, opp_table, out, turned, held, flat):
    core = lax.axis_index("beta")
    held[core] = own[...]
    held[1 - core] = other[...]
    for kind in range(table.shape[0]):
        flat[kind] = table[kind].T
        turned[kind] = opp_table[kind].T

    def body(tile, carry):
        cols = pl.ds(pl.multiple_of(tile * TILE, TILE), TILE)
        out[:, cols] = beta_tile(held, flat, sources, kinds, tile, links)
        return carry

    lax.fori_loop(0, out.shape[1] // TILE, body, 0, unroll=16)


def same_part(sources, kinds, own, other, table, opp_table):
    rows, cols = own.shape
    return pl.pallas_call(
        functools.partial(same_kernel, sources.shape[1]),
        out_shape=[
            jax.ShapeDtypeStruct((rows, cols), jnp.float32),
            jax.ShapeDtypeStruct(opp_table.shape, opp_table.dtype),
        ],
        in_specs=[SMEM] * 2 + [VMEM] * 4,
        out_specs=[VMEM] * 2,
        scratch_shapes=[
            pltpu.VMEM((2, rows, cols), own.dtype),
            pltpu.VMEM(table.shape, table.dtype),
        ],
        cost_estimate=cost(0, rows * cols),
        compiler_params=pltpu.CompilerParams(vmem_limit_bytes=LIMIT),
        name="same",
    )(sources, kinds, own, other, table, opp_table)


def mixed_kernel(links, sources, kinds, table, start, mark, *rest):
    half, other, alpha = rest[:RING], rest[RING : 2 * RING], rest[2 * RING : 3 * RING]
    out, held, added = rest[3 * RING :]
    spot, core = lax.axis_index("ring"), lax.axis_index("beta")
    for d in range(RING):
        quarter = lax.bitwise_xor(spot, d)
        held[core * RING + quarter] = half[d][...]
        held[(1 - core) * RING + quarter] = other[d][...]
        added[quarter] = alpha[d][...]
    per_piece = held.shape[2] // TILE

    def body(tile, carry):
        cols = pl.ds(pl.multiple_of(tile * TILE, TILE), TILE)
        part = pl.ds(pl.multiple_of(lax.rem(tile, per_piece) * TILE, TILE), TILE)
        total = beta_tile(held, table, sources, kinds, tile, links) + start[:, cols]
        total = total + added[lax.div(tile, per_piece), :, part].astype(jnp.float32)
        out[:, cols] = total.astype(out.dtype)
        return carry

    lax.fori_loop(0, out.shape[1] // TILE, body, 0, unroll=16)


def mixed_part(sources, kinds, table, start, mark, half, other, alpha):
    rows, cols = start.shape
    kind = half[0].dtype
    return pl.pallas_call(
        functools.partial(mixed_kernel, sources.shape[1]),
        out_shape=jax.ShapeDtypeStruct((rows, cols), kind),
        in_specs=[SMEM] * 2 + [VMEM] * 2 + [ANY] + [VMEM] * (3 * RING),
        out_specs=VMEM,
        scratch_shapes=[
            pltpu.VMEM((2 * RING, rows, cols // RING), kind),
            pltpu.VMEM((RING, rows, cols // RING), kind),
        ],
        cost_estimate=cost(0, rows * cols),
        compiler_params=pltpu.CompilerParams(vmem_limit_bytes=LIMIT),
        name="mixed",
    )(sources, kinds, table, start, mark, *half, *other, *alpha)


def mark_kernel(*refs):
    refs[-1][...] = jnp.zeros_like(refs[-1])


def marked(pieces):
    return pl.pallas_call(
        mark_kernel,
        out_shape=jax.ShapeDtypeStruct((8, TILE), jnp.float32),
        in_specs=[ANY] * len(pieces),
        out_specs=VMEM,
        cost_estimate=cost(0, MARK),
        compiler_params=pltpu.CompilerParams(vmem_limit_bytes=LIMIT),
        name="mark",
    )(*pieces)


def swapped(value, axis, flip):
    return lax.ppermute(value, axis, [(i, i ^ flip) for i in range(lax.axis_size(axis))])


def exchanged(pieces):
    return [pieces[0]] + [swapped(pieces[d], "ring", d) for d in range(1, RING)]


def handed(value, parity):
    count = lax.axis_size("row")
    pairs = [(row, row + 1) for row in range(parity, count - 1, 2)]
    return lax.ppermute(value, "row", pairs + [(there, here) for here, there in pairs])


def local(
    coeffs,
    beta_list,
    beta_kind,
    opp_beta_kind,
    alpha_list,
    alpha_kind,
    opp_list,
    opp_kind,
    beta_table,
    alpha_table,
    opp_alpha_table,
    opp_beta_table,
):
    own = coeffs[0]
    row = lax.axis_index("row")

    def mine(lists):
        return lax.dynamic_slice_in_dim(lists, row * RING, RING, 0)

    near_lists = [mine(part) for part in (opp_list, opp_kind, alpha_list, alpha_kind)]
    pieces = exchanged(cut(own))
    other = swapped(own, "beta", 1)
    same, turned = same_part(
        beta_list, beta_kind, own, other, beta_table, opp_beta_table
    )
    even, odd = edges(pieces)
    even, odd = handed(even, 0), handed(odd, 1)
    even, odd, same, near_lists = lax.optimization_barrier((even, odd, same, near_lists))
    half = exchanged(near(*near_lists[:2], pieces, even, odd, opp_alpha_table, "half"))
    formed = near(*near_lists[2:], pieces, even, odd, alpha_table, "alpha")
    half = [half[d] for d in (0, 2, 1, 3)]
    half, mark = lax.optimization_barrier((half, formed[0]))
    half = [half[d] for d in (0, 2, 1, 3)]
    alpha = exchanged(formed)
    half_other = [swapped(piece, "beta", 1) for piece in half]
    mark = marked([alpha[d] for d in (1, 3, 2)])
    total = mixed_part(
        beta_list, opp_beta_kind, turned, same, mark, half, half_other, alpha
    )
    return total[None]


def solution(mesh):
    split = Mesh(
        mesh.devices.reshape(-1, RING, mesh.devices.shape[1]), ("row", "ring", "beta")
    )
    vector = P(None, ("row", "ring"), "beta")
    lists = P("beta", None)
    placed = (vector, lists, lists, lists) + (P(),) * 8
    return jax.shard_map(
        local, mesh=split, in_specs=placed, out_specs=vector, check_vma=False
    )
```
